512 devices in a mesh: ep: 128 (over z, x, core), tp: 4 (over y).
Axes of the slice: x: 4, y: 4, z: 16, core: 2. Of those that a mesh axis runs over, the one named last changes fastest.
Arguments:
- attn_out: bfloat16 [16384, 1536], P('ep', 'tp'), may hold values from -6 to 6
- residual: bfloat16 [16384, 1536], P('ep'), may hold values from -6 to 6
- w_out: bfloat16 [1536, 1536], P('tp'), may hold values from -0.15625 to 0.15625
- w_router: bfloat16 [1536, 40], replicated, may hold values from -0.25 to 0.25
- expert_ids: int32 [16384, 8], P('ep'), may hold values from 0 to 39, as said below
- slot_expert: int32 [128], replicated, may hold values from 0 to 39, as said below
- w_in: bfloat16 [128, 1536, 2, 512], P('ep', None, None, 'tp')
- w_down: bfloat16 [128, 512, 1536], P('ep', None, 'tp')
- norm_gain: float32 [1536], P('tp'), may hold values from 0.25 to 1.75
Outputs:
- normed: bfloat16 [16384, 1536], P('ep', 'tp')
The draws below stay inside these ranges and needn't reach their ends.
Inputs may be any that keep to these rules, and one draw needn't show every extreme that they name: `slot_expert`: every expert fills at least one and at most four slots; all slots of one expert hold equal w_in and w_down. `expert_ids`: each row names 8 different experts. Within each aligned block of 128 rows, expert e is named by at most 10 * copies[e] rows, and one expert reaches that bound in every block.
All inputs are finite; a program needn't handle non-finite values.
Results may differ from the reference program's by a relative error of at most 0.0067.
Values may be sent and summed in bfloat16 or wider, within the bound.
No kernel may reach another device: no remote copies, remote signals or barrier semaphores. Data moves between devices by JAX's collectives and lax.ppermute only.
A program may use at most 64 MiB of HBM per device.

```python
import jax
import jax.numpy as jnp
from jax import lax

D = 1536
FF = 512
E = 40
TOPK = 8
ROWS_DEV = 128
ROWS = 16384
SLOTS = 128
CAP = 10
N_EP = 128


def slot_table(key):
    order = jax.random.permutation(jax.random.fold_in(key, 11), E).astype(jnp.int32)
    extra = SLOTS - E
    hot = max(1, min(E, (extra + 2) // 3))
    extra_ids = order[jnp.arange(extra, dtype=jnp.int32) % hot]
    listed = jnp.concatenate([jnp.arange(E, dtype=jnp.int32), extra_ids.astype(jnp.int32)])
    mixing = jax.random.permutation(jax.random.fold_in(key, 12), SLOTS)
    return listed[mixing].astype(jnp.int32)


def feature_marks(key):
    picked = jax.random.permutation(jax.random.fold_in(key, 31), D)[:4].astype(jnp.int32)
    columns = jnp.arange(D, dtype=jnp.int32)
    return jnp.any(columns[:, None] == picked[None, :], axis=1)


def draw_slot_expert(key, part):
    return slot_table(key)


def draw_expert_ids(key, part):
    table = slot_table(key)
    chosen = table[0]
    units = SLOTS * CAP
    unit_expert = table[jnp.arange(units, dtype=jnp.int32) // CAP]

    def one_block(block_key):
        scores = jax.random.permutation(block_key, units).astype(jnp.int32)
        scores = jnp.where(unit_expert == chosen, scores - units, scores)
        order = jnp.argsort(scores, stable=True)
        kept = jnp.sort(unit_expert[order[:ROWS_DEV * TOPK]])
        grid = kept.reshape(TOPK, ROWS_DEV).T
        grid = grid[jax.random.permutation(jax.random.fold_in(block_key, 1), ROWS_DEV)]
        noise = jax.random.randint(jax.random.fold_in(block_key, 2), (ROWS_DEV, TOPK), 0, 1 << 20) * TOPK
        noise = noise + jnp.arange(TOPK, dtype=jnp.int32)[None, :]
        columns = jnp.argsort(noise, axis=1)
        return jnp.take_along_axis(grid, columns, axis=1)
    block_keys = jax.random.split(jax.random.fold_in(key, 13), ROWS // ROWS_DEV)
    return jax.vmap(one_block)(block_keys).reshape(ROWS, TOPK).astype(jnp.int32)


def draw_residual(key, part):
    marks = feature_marks(key)
    base = jnp.clip(jax.random.normal(jax.random.fold_in(key, 32), (ROWS, D), jnp.float32), -6.0, 6.0)
    level = jax.random.uniform(jax.random.fold_in(key, 33), (ROWS, D), jnp.float32, 4.5, 5.5)
    return jnp.where(marks[None, :], level, base).astype(jnp.bfloat16)


def draw_w_router(key, part):
    marks = feature_marks(key)
    favoured = jax.random.permutation(jax.random.fold_in(key, 34), E)[:E // 5].astype(jnp.int32)
    kinds = jnp.arange(E, dtype=jnp.int32)
    strong = jnp.any(kinds[:, None] == favoured[None, :], axis=1)
    spread = 0.2 * D ** (-0.5)
    base = jnp.clip(jax.random.normal(jax.random.fold_in(key, 35), (D, E), jnp.float32), -4.0, 4.0) * spread
    weak_level = jax.random.uniform(jax.random.fold_in(key, 36), (D, E), jnp.float32, -0.22, -0.18)
    strong_level = jax.random.uniform(jax.random.fold_in(key, 37), (D, E), jnp.float32, -0.02, 0.02)
    marked = jnp.where(strong[None, :], strong_level, weak_level)
    return jnp.where(marks[:, None], marked, base).astype(jnp.bfloat16)


def draw_w_in(key, part):
    table = slot_table(key)
    experts = jax.random.normal(jax.random.fold_in(key, 21), (E, D, 2, FF), jnp.float32) * D ** (-0.5)
    return experts[table].astype(jnp.bfloat16)


def draw_w_down(key, part):
    table = slot_table(key)
    experts = jax.random.normal(jax.random.fold_in(key, 22), (E, FF, D), jnp.float32) * (3.0 * FF ** (-0.5))
    return experts[table].astype(jnp.bfloat16)


def level_of(stream_key, dims, cuts, smallest, top_value):
    gain = 1.0
    for position, blocks in cuts:
        steps = jax.random.uniform(jax.random.fold_in(jax.random.fold_in(stream_key, 6), position), (blocks,), jnp.float32, smallest / len(cuts), top_value / len(cuts))
        gain = gain * jnp.repeat(jnp.exp(steps), dims[position] // blocks).reshape((-1,) + (1,) * (len(dims) - 1 - position))
    return gain


def centred(key, shape, deviation, bound, cuts=(), kind=jnp.bfloat16):
    array = deviation * jax.random.normal(key, shape, jnp.float32)
    if cuts:
        array = array * level_of(key, shape, cuts, -0.22, 0.18)
    return jnp.clip(array, -bound, bound).astype(kind)


def setup_inputs(seed: int = 0) -> dict:
    key_list = jax.random.split(jax.random.key(seed), 10)
    return {
        "attn_out": centred(key_list[0], (ROWS, D), 1.0, 6.0, ((0, 128), (1, 4))),
        "residual": draw_residual(jax.random.fold_in(key_list[9], 71), 0),
        "w_out": centred(key_list[2], (D, D), D ** -0.5, 0.15625, ((0, 4),)),
        "w_router": draw_w_router(jax.random.fold_in(key_list[9], 71), 0),
        "expert_ids": draw_expert_ids(jax.random.fold_in(key_list[9], 71), 0),
        "slot_expert": draw_slot_expert(jax.random.fold_in(key_list[9], 71), 0),
        "w_in": draw_w_in(jax.random.fold_in(key_list[9], 71), 0),
        "w_down": draw_w_down(jax.random.fold_in(key_list[9], 71), 0),
        "norm_gain": jnp.clip(1.0 + 0.15 * jax.random.normal(key_list[8], (D,), jnp.float32), 0.25, 1.75),
    }


def route(ids, slot_expert, capacity):
    flat = ids.reshape(-1)
    kinds = jnp.arange(E, dtype=jnp.int32)
    onehot = (flat[:, None] == kinds[None, :]).astype(jnp.int32)
    before = jnp.cumsum(onehot, axis=0) - onehot
    rank = lax.optimization_barrier(jnp.sum(before * onehot, axis=1))
    slot_hot = (slot_expert[:, None] == kinds[None, :]).astype(jnp.int32)
    copies = lax.optimization_barrier(jnp.sum(slot_hot, axis=0))
    copy_no = lax.optimization_barrier(jnp.sum((jnp.cumsum(slot_hot, axis=0) - slot_hot) * slot_hot, axis=1))
    mine = lax.optimization_barrier(jnp.sum(onehot * copies[None, :], axis=1))
    copy_pick = rank % mine
    place = rank // mine
    match = (slot_expert[None, :] == flat[:, None]) & (copy_no[None, :] == copy_pick[:, None])
    slot_ids = jnp.arange(slot_expert.shape[0], dtype=jnp.int32)
    slot = lax.optimization_barrier(jnp.sum(jnp.where(match, slot_ids[None, :], 0), axis=1)).astype(jnp.int32)
    return (slot * capacity + place).astype(jnp.int32)

def reference(attn_out, residual, w_out, w_router, expert_ids, slot_expert, w_in, w_down, norm_gain):
    proj = jnp.dot(attn_out, w_out, preferred_element_type=jnp.float32)
    stream = (residual.astype(jnp.float32) + proj).astype(jnp.bfloat16)
    logits = jnp.dot(stream, w_router, preferred_element_type=jnp.float32)
    picked = jnp.take_along_axis(logits, expert_ids, axis=1)
    weights = jnp.exp(picked)
    gates = weights / lax.optimization_barrier(jnp.sum(weights, axis=1, keepdims=True))
    blocks = expert_ids.reshape(N_EP, ROWS_DEV, TOPK)

    def block_route(ids):
        return route(ids, slot_expert, CAP)
    dest = jax.vmap(block_route)(blocks)
    assigns = ROWS_DEV * TOPK
    source = jnp.arange(N_EP, dtype=jnp.int32)[:, None]
    row_ids = source * ROWS_DEV + jnp.arange(assigns, dtype=jnp.int32)[None, :] // TOPK
    source_all = jnp.broadcast_to(source, (N_EP, assigns))
    table = jnp.zeros((N_EP, SLOTS * CAP), jnp.int32).at[source_all, dest].set(row_ids)
    gate_table = jnp.zeros((N_EP, SLOTS * CAP), jnp.float32).at[source_all, dest].set(gates.reshape(N_EP, assigns))

    def per_slot(total, slot):
        start = (slot * CAP).astype(jnp.int32)
        zero = jnp.zeros((), jnp.int32)
        index = lax.dynamic_slice(table, (zero, start), (N_EP, CAP))
        gate = lax.dynamic_slice(gate_table, (zero, start), (N_EP, CAP))
        rows_in = stream[index].astype(jnp.float32)
        gu = jnp.einsum('nce,egf->ncgf', rows_in, w_in[slot].astype(jnp.float32))
        hidden = (jax.nn.silu(gu[:, :, 0]) * gu[:, :, 1]).astype(jnp.bfloat16)
        outs = jnp.einsum('ncf,fd->ncd', hidden.astype(jnp.float32), w_down[slot].astype(jnp.float32)).astype(jnp.bfloat16)
        added = (gate[:, :, None] * outs.astype(jnp.float32)).reshape(N_EP * CAP, D)
        return (total.at[index.reshape(-1)].add(added), None)
    moe, _ = lax.scan(per_slot, jnp.zeros((ROWS, D), jnp.float32), jnp.arange(SLOTS, dtype=jnp.int32))
    mixed = stream.astype(jnp.float32) + moe
    square = lax.optimization_barrier(jnp.mean(mixed * mixed, axis=1, keepdims=True))
    return (mixed * lax.rsqrt(square + 1e-06) * norm_gain[None, :]).astype(jnp.bfloat16)
```

```python
import jax
import jax.numpy as jnp
import numpy as np
from jax import lax
from jax.sharding import Mesh, PartitionSpec as P

E = 40
NZ, NX, NC, NY = 16, 4, 2, 4
NXC = NX * NC
ZS = NZ // NY
XCY = ("x", "c", "y")


def swap(x, axis):
    return lax.all_to_all(x, axis, 0, 0, tiled=True)


def sum_over_y(x):
    return jnp.sum(swap(jnp.broadcast_to(x[None], (NY,) + x.shape), "y"), axis=0)


def slot_tables(slot_expert, capacity):
    slots = slot_expert.shape[0]
    kinds = jnp.arange(E, dtype=jnp.int32)
    number = jnp.arange(slots, dtype=jnp.int32)
    same = slot_expert[:, None] == slot_expert[None, :]
    copies = jnp.sum(same.astype(jnp.int32), axis=1)
    copy_no = jnp.sum((same & (number[None, :] < number[:, None])).astype(jnp.int32), axis=1)
    hot = (slot_expert[:, None] == kinds[None, :]).astype(jnp.bfloat16)
    place = jnp.arange(capacity, dtype=jnp.int32)
    wanted = place[None, :] * copies[:, None] + copy_no[:, None]
    hot_q = jnp.broadcast_to(hot[:, None, :], (slots, capacity, E)).reshape(slots * capacity, E)
    return hot_q, wanted.reshape(slots * capacity)


def per_device(
    attn_out, residual, w_out, w_router, expert_ids, slot_expert, w_in, w_down, norm_gain
):
    rows, quarter = attn_out.shape
    width = residual.shape[1]
    topk = expert_ids.shape[1]
    slots = slot_expert.shape[0]
    capacity = (rows * topk * 5 // 4 + slots - 1) // slots
    total = slots * capacity
    per_z = NXC * capacity
    part = ZS * capacity
    served = NXC * part
    tp_pos = lax.axis_index("y")
    ff_part = w_in.shape[3]

    win_all = lax.all_gather(w_in.reshape(width, 2 * ff_part), "y")
    wdown_all = lax.all_gather(w_down[0], "y")

    partial_value = jnp.einsum(
        "rk,kqd->qrd", attn_out, w_out.reshape(quarter, NY, quarter),
        preferred_element_type=jnp.float32,
    )
    proj = jnp.sum(swap(partial_value, "y"), axis=0)
    mine = lax.dynamic_slice_in_dim(residual, tp_pos * quarter, quarter, 1)
    stream = (mine.astype(jnp.float32) + proj).astype(jnp.bfloat16)

    kinds = jnp.arange(E, dtype=jnp.int32)
    member = jnp.any(expert_ids[:, :, None] == kinds[None, None, :], axis=1)
    row_no = jnp.arange(rows, dtype=jnp.int32)
    earlier = (row_no[None, :] < row_no[:, None]).astype(jnp.bfloat16)
    rank = jnp.dot(earlier, member.astype(jnp.bfloat16), preferred_element_type=jnp.float32)
    rank = jnp.where(member, rank, -1.0).astype(jnp.bfloat16)
    hot_q, wanted = slot_tables(slot_expert, capacity)
    rank_q = lax.dot_general(
        hot_q, rank, (((1,), (1,)), ((), ())), preferred_element_type=jnp.float32
    )
    pick = rank_q == wanted.astype(jnp.float32)[:, None]
    send = jnp.dot(pick.astype(jnp.bfloat16), stream, preferred_element_type=jnp.float32)
    send = send.astype(jnp.bfloat16).reshape(NZ, per_z, quarter)
    came = swap(send, "z")
    came = came.reshape(NY, ZS, NXC, capacity, quarter).transpose(2, 0, 1, 3, 4)
    came = swap(came.reshape(NXC * NY, part, quarter), XCY)
    tokens = came.reshape(NXC, NY, part, quarter).transpose(0, 2, 1, 3).reshape(served, width)

    router_part = lax.dynamic_slice_in_dim(w_router, tp_pos * quarter, quarter, 0)
    logits = sum_over_y(jnp.dot(stream, router_part, preferred_element_type=jnp.float32))
    weights = jnp.where(member, jnp.exp(logits), 0.0)
    gates = weights / jnp.sum(weights, axis=1, keepdims=True)
    gates_hi = gates.astype(jnp.bfloat16)
    gates_lo = (gates - gates_hi.astype(jnp.float32)).astype(jnp.bfloat16)

    gu = jnp.einsum("rd,udc->urc", tokens, win_all, preferred_element_type=jnp.float32)
    hidden = (jax.nn.silu(gu[..., :ff_part]) * gu[..., ff_part:]).astype(jnp.bfloat16)
    hidden = hidden.transpose(1, 0, 2).reshape(served, NY * ff_part)
    outs = jnp.einsum("rf,tfd->trd", hidden, wdown_all, preferred_element_type=jnp.float32)
    outs = outs.astype(jnp.bfloat16).reshape(NY, NXC, part, quarter).transpose(1, 0, 2, 3)
    back = swap(outs.reshape(NXC * NY, part, quarter), XCY)
    back = back.reshape(NXC, NY, ZS, capacity, quarter).transpose(1, 2, 0, 3, 4)
    back = swap(back.reshape(NZ, per_z, quarter), "z").reshape(total, quarter)

    def weigh(part_of_gates):
        spread = lax.dot_general(
            hot_q, part_of_gates, (((1,), (1,)), ((), ())), preferred_element_type=jnp.float32
        )
        spread = jnp.where(pick, spread, 0.0).astype(jnp.bfloat16)
        return lax.dot_general(
            spread, back, (((0,), (0,)), ((), ())), preferred_element_type=jnp.float32
        )

    mixed = stream.astype(jnp.float32) + (weigh(gates_hi) + weigh(gates_lo))
    square = sum_over_y(jnp.sum(mixed * mixed, axis=1)[None, :])[0]
    scale = lax.rsqrt(square / width + 1e-06)
    return (mixed * scale[:, None] * norm_gain[None, :]).astype(jnp.bfloat16)


def solution(mesh):
    fine = Mesh(mesh.devices.reshape(NZ, NX, NC, NY), ("z", "x", "c", "y"))
    ep = ("z", "x", "c")
    return jax.shard_map(
        per_device,
        mesh=fine,
        in_specs=(
            P(ep, "y"),
            P(ep, None),
            P("y", None),
            P(),
            P(ep, None),
            P(),
            P(ep, None, None, "y"),
            P(ep, None, "y"),
            P("y"),
        ),
        out_specs=P(ep, "y"),
        check_vma=False,
    )
```
